32 devices in a mesh: dp: 8 (over y, x, core), tensor: 4 (over z).
Axes of the slice: x: 2, y: 2, z: 4, core: 2. Of those that a mesh axis runs over, the one named last changes fastest.
Arguments:
- layer_inputs: bfloat16 [256, 8192], P(None, ('dp', 'tensor')), may hold values from -6 to 6
- policy_query_weight: bfloat16 [8192, 8192], P('dp', 'tensor'), may hold values from -0.0625 to 0.0625
- policy_key_value: bfloat16 [8192, 8, 256], P('dp', 'tensor'), may hold values from -0.0625 to 0.0625
- policy_out: bfloat16 [8192, 8192], P('tensor', 'dp'), may hold values from -0.0625 to 0.0625
- kv_cache: bfloat16 [256, 256, 8, 256], P('dp', None, 'tensor'), may hold values from -400 to 400
- prefix_len: int32 [256], P('dp'), may hold values from 1 to 256, 32768 in all
- responses: bfloat16 [128, 16, 8192], P('dp'), may hold values from -11 to 11
- response_len: int32 [128], P('dp'), may hold values from 1 to 16, 1024 in all
- assign: int32 [128, 1], P('dp'), may hold values from 0 to 7; in each aligned block of 16 rows (0 to 15, 16 to 31, ...) at most 2 rows name the same one
- critic_query_weight: bfloat16 [8192, 8192], P('dp', 'tensor'), may hold values from -1 to 1
- critic_key_value: bfloat16 [8192, 8, 256], P('dp', 'tensor'), may hold values from -1 to 1
- score_weight: bfloat16 [8192], P('tensor'), may hold values from -0.0625 to 0.0625
Outputs:
- decode_out: bfloat16 [2, 256, 8192], P(None, None, ('dp', 'tensor'))
- values: float32 [8, 16, 16], P('dp')
The draws below stay inside these ranges and needn't reach their ends.
Inputs may be any that keep to these rules, and one draw needn't show every extreme that they name: `assign`: within the rows of one dp device at most 2 rows name the same shard, and this bound is reached.
All inputs are finite; a program needn't handle non-finite values. No bound on the sum of `prefix_len` or of `response_len` on one device may be relied on, other than what follows from the above.
Results may differ from the reference program's by a relative error of at most 0.0078.
Values may be sent and summed in bfloat16 or wider, within the bound.
No kernel may reach another device: no remote copies, remote signals or barrier semaphores. Data moves between devices by JAX's collectives and lax.ppermute only.
A program may use at most 192 MiB of HBM per device.

```python
import math
import jax
import jax.numpy as jnp
import numpy as np
from jax import lax

MODEL_DIM = 8192
QUERY_HEADS = 64
KEY_HEADS = 8
HEAD_DIM = 128
STEPS = 2
CAPR = 2
CACHE_LENGTH = 256
RR = 16
RESPONSE_LENGTH = 16
DECODE_ROWS = 256
RESPONSE_ROWS = 128
N_DP = 8


def draw_kv_cache(key, part):
    base_offset = jnp.clip(jax.random.normal(key, (DECODE_ROWS, CACHE_LENGTH, KEY_HEADS, 2 * HEAD_DIM), jnp.float32), -6.0, 6.0)
    return base_offset.astype(jnp.bfloat16)


def critic_draw(key):
    group_index = QUERY_HEADS // KEY_HEADS
    inverse = MODEL_DIM ** (-0.5)
    token_noise = jnp.clip(jax.random.normal(jax.random.fold_in(key, 31), (RESPONSE_ROWS, RESPONSE_LENGTH, MODEL_DIM), jnp.float32), -6.0, 6.0)
    query_jitter = jnp.clip(jax.random.normal(jax.random.fold_in(key, 32), (MODEL_DIM, KEY_HEADS, group_index, HEAD_DIM), jnp.float32), -6.0, 6.0)
    pair_jitter = jnp.clip(jax.random.normal(jax.random.fold_in(key, 33), (MODEL_DIM, KEY_HEADS, 2 * HEAD_DIM), jnp.float32), -6.0, 6.0)
    weight_q = query_jitter * inverse
    weight_kv = pair_jitter * inverse
    token_rows = token_noise
    return (token_rows, weight_q.reshape(MODEL_DIM, QUERY_HEADS * HEAD_DIM), weight_kv)


def draw_responses(key, part):
    return critic_draw(key)[0].astype(jnp.bfloat16)


def draw_critic_query_weight(key, part):
    return critic_draw(key)[1].astype(jnp.bfloat16)


def draw_critic_key_value(key, part):
    return critic_draw(key)[2].astype(jnp.bfloat16)


def shard_levels(key, extent, pieces, least, largest):
    gain, own = 1.0, jax.random.fold_in(key, 6)
    for position, parts in pieces:
        steps = jnp.exp(jax.random.uniform(jax.random.fold_in(own, position), (parts,), jnp.float32, least / len(pieces), largest / len(pieces)))
        gain = gain * jnp.repeat(steps, extent[position] // parts).reshape([-1 if axis == position else 1 for axis in range(len(extent))])
    return gain


def length_profile(number_of, total, most, lean):
    portions = [(1 << 20) // math.isqrt(rank ** lean) + 1 for rank in range(2, number_of + 1)]
    spare, counts = total - most - (number_of - 1), [1] * (number_of - 1)
    while spare > 0:
        free = [i for i in range(number_of - 1) if counts[i] < most]
        whole, left = sum([portions[i] for i in free]), spare
        for i in free:
            extra = min(most - counts[i], max(1, left * portions[i] // whole), spare)
            counts[i] = counts[i] + extra
            spare = spare - extra
    return np.array([most] + counts)


def ragged(rng, amount, total, most, lean):
    if amount == 2:
        one = jax.random.randint(rng, (), max(1, total - most), min(most, total - 1) + 1)
        return jnp.stack([one, total - one])
    sizes = jnp.asarray(length_profile(amount, total, most, lean), jnp.int32)
    twos = (amount - 1) // 2
    donor, receiver = sizes[1:1 + 2 * twos:2], sizes[2:2 + 2 * twos:2]
    margin = jnp.minimum(donor - 1, most - receiver)
    passed = jax.random.randint(jax.random.fold_in(rng, 1), (twos,), 0, 1 << 20) % (margin + 1)
    sizes = sizes.at[1:1 + 2 * twos:2].set(donor - passed).at[2:2 + 2 * twos:2].set(receiver + passed)
    return sizes[jax.random.permutation(jax.random.fold_in(rng, 2), amount)]


def assign_block(own_key, own, number, rows, number_of, top, most, slope):
    sequence = jax.random.permutation(own_key, number_of)
    crowded, ordinary = portions_of(number_of, rows * top, most, slope, True), portions_of(number_of, rows * top, most, slope, False)
    places = jnp.arange(number_of)

    def named(lengths, offset_by):
        used = int((lengths > 0).sum())
        fixed = max(1, used // 4)
        shifted = fixed + (places - fixed + offset_by * (used - fixed)) % max(1, number_of - fixed)
        return jnp.zeros((number_of,), jnp.int32).at[sequence[jnp.where(places < fixed, places, shifted)]].set(jnp.asarray(lengths, jnp.int32))

    lengths = jnp.where(number % 4 == 0, named(crowded, number // 4), named(ordinary, number - number // 4 - 1))
    mixed = jax.random.permutation(jax.random.fold_in(own, 3), number_of)
    donor, sink = mixed[0:number_of // 2 * 2:2], mixed[1:number_of // 2 * 2:2]
    slack = jnp.minimum(lengths[donor] - 1, most - lengths[sink]) // 2
    slack = jnp.where((donor == sequence[0]) | (sink == sequence[0]) | (lengths[sink] == 0), 0, jnp.maximum(slack, 0))
    shifted = jax.random.randint(jax.random.fold_in(own, 4), (number_of // 2,), 0, 1 << 20) % (slack + 1)
    lengths = lengths.at[donor].add(-shifted).at[sink].add(shifted)
    labels = jnp.searchsorted(jnp.cumsum(lengths), jnp.arange(rows * top), side="right").astype(jnp.int32)
    table = labels.reshape(top, rows).T
    table = table[jax.random.permutation(jax.random.fold_in(own, 1), rows)]
    offset_by = jax.random.randint(jax.random.fold_in(own, 2), (rows, 1), 0, top)
    return jnp.take_along_axis(table, (jnp.arange(top)[None, :] + offset_by) % top, axis=1)


def portions_of(number_of, total, reach, slope, full):
    weights = [(1 << 20) // math.isqrt(grade ** slope) + 1 for grade in range(1, number_of + 1)]
    largest = reach if full else min(reach, max(-(-total // number_of), total * weights[0] // sum(weights)))
    least = 1 if total - largest >= number_of - 1 else 0
    holding, rest = [largest] + [least] * (number_of - 1), total - largest - least * (number_of - 1)
    while rest > 0:
        movable = [i for i in range(1, number_of) if holding[i] < largest] or [i for i in range(1, number_of) if holding[i] < reach]
        pool, left = sum([weights[i] for i in movable]), rest
        for i in movable:
            addition = min(reach - holding[i], max(1, left * weights[i] // pool), rest)
            holding[i] = holding[i] + addition
            rest = rest - addition
    return np.array(holding)


def normal_values(own_key, dims, scale, most, split=(), kind=jnp.bfloat16):
    factor_of = shard_levels(own_key, dims, split, -0.22, 0.18) if split else 1.0
    drawn = jax.random.normal(own_key, dims, jnp.float32) * scale * factor_of
    return jnp.minimum(jnp.maximum(drawn, -most), most).astype(kind)


def setup_inputs(seed: int = 0) -> dict:
    key_list = jax.random.split(jax.random.key(seed), 13)
    layer_inputs = normal_values(key_list[0], (DECODE_ROWS, MODEL_DIM), 1.0, 6.0, ((1, 32),))
    policy_query_weight = normal_values(key_list[1], (MODEL_DIM, QUERY_HEADS * HEAD_DIM), MODEL_DIM ** -0.5, 0.0625, ((0, 8), (1, 4)))
    policy_key_value = normal_values(key_list[2], (MODEL_DIM, KEY_HEADS, 2 * HEAD_DIM), MODEL_DIM ** -0.5, 0.0625, ((0, 8), (1, 4)))
    policy_out = normal_values(key_list[3], (QUERY_HEADS * HEAD_DIM, MODEL_DIM), (QUERY_HEADS * HEAD_DIM) ** -0.5, 0.0625, ((0, 4), (1, 8)))
    kv_cache = draw_kv_cache(jax.random.fold_in(key_list[12], 71), 0)
    prefix_len = ragged(key_list[5], DECODE_ROWS, DECODE_ROWS * CACHE_LENGTH // 2, CACHE_LENGTH, 1).astype(jnp.int32)
    responses = draw_responses(jax.random.fold_in(key_list[12], 71), 0)
    response_len = ragged(key_list[7], RESPONSE_ROWS, RESPONSE_ROWS * RESPONSE_LENGTH // 2, RESPONSE_LENGTH, 1).astype(jnp.int32)
    assign_keys = jax.random.split(jax.random.fold_in(key_list[8], 1), RESPONSE_ROWS // RR)
    assign_turns = jax.random.permutation(jax.random.fold_in(key_list[8], 3), RESPONSE_ROWS // RR)
    assign = jax.vmap(lambda own, number: assign_block(jax.random.fold_in(key_list[8], 2), own, number, RR, N_DP, 1, CAPR, 2))(assign_keys, assign_turns).reshape((RESPONSE_ROWS, 1))
    critic_query_weight = draw_critic_query_weight(jax.random.fold_in(key_list[12], 71), 0)
    critic_key_value = draw_critic_key_value(jax.random.fold_in(key_list[12], 71), 0)
    score_weight = normal_values(key_list[11], (QUERY_HEADS * HEAD_DIM,), (QUERY_HEADS * HEAD_DIM) ** -0.5, 0.0625, ((0, 4),))
    return dict(layer_inputs=layer_inputs, policy_query_weight=policy_query_weight, policy_key_value=policy_key_value, policy_out=policy_out, kv_cache=kv_cache, prefix_len=prefix_len, responses=responses, response_len=response_len, assign=assign, critic_query_weight=critic_query_weight, critic_key_value=critic_key_value, score_weight=score_weight)


def reference(layer_inputs, policy_query_weight, policy_key_value, policy_out, kv_cache, prefix_len, responses, response_len, assign, critic_query_weight, critic_key_value, score_weight):
    group_index = QUERY_HEADS // KEY_HEADS
    scale_factor = HEAD_DIM ** -0.5
    cache_keys = kv_cache[..., :HEAD_DIM].astype(jnp.float32)
    cache_values = kv_cache[..., HEAD_DIM:].astype(jnp.float32)
    cache_mask = lax.broadcasted_iota(jnp.int32, (DECODE_ROWS, CACHE_LENGTH), 1) < prefix_len[:, None]
    current_state = layer_inputs
    fresh_entries = []
    outputs = []
    for step in range(STEPS):
        query_rows = jnp.dot(current_state, policy_query_weight, preferred_element_type=jnp.float32).astype(jnp.bfloat16).reshape(DECODE_ROWS, KEY_HEADS, group_index, HEAD_DIM).astype(jnp.float32)
        fresh_entries.append(jnp.dot(current_state, policy_key_value.reshape(MODEL_DIM, -1), preferred_element_type=jnp.float32).astype(jnp.bfloat16).reshape(DECODE_ROWS, KEY_HEADS, 2 * HEAD_DIM))
        fresh_all = jnp.stack(fresh_entries)
        new_keys = fresh_all[:, :, :, :HEAD_DIM].astype(jnp.float32)
        new_values = fresh_all[:, :, :, HEAD_DIM:].astype(jnp.float32)
        old_scores = jnp.einsum('rkgd,rckd->rkgc', query_rows, cache_keys) * scale_factor
        old_scores = jnp.where(cache_mask[:, None, None, :], old_scores, -1e30)
        new_scores = jnp.einsum('rkgd,trkd->rkgt', query_rows, new_keys) * scale_factor
        top = jnp.maximum(jnp.max(old_scores, -1), jnp.max(new_scores, -1))
        old_exp = jnp.exp(old_scores - top[..., None])
        new_exp = jnp.exp(new_scores - top[..., None])
        total = jnp.sum(old_exp, -1) + jnp.sum(new_exp, -1)
        old_weights = (old_exp / total[..., None]).astype(jnp.bfloat16).astype(jnp.float32)
        new_weights = (new_exp / total[..., None]).astype(jnp.bfloat16).astype(jnp.float32)
        mixed = jnp.einsum('rkgc,rckd->rkgd', old_weights, cache_values) + jnp.einsum('rkgt,trkd->rkgd', new_weights, new_values)
        attended = mixed.astype(jnp.bfloat16).reshape(DECODE_ROWS, -1)
        summed = jnp.dot(attended, policy_out, preferred_element_type=jnp.float32)
        current_state = (current_state.astype(jnp.float32) + summed).astype(jnp.bfloat16)
        outputs.append(current_state)
    decode_out = jnp.stack(outputs)

    token_rows = responses.reshape(-1, MODEL_DIM)
    critic_query_rows = jnp.dot(token_rows, critic_query_weight, preferred_element_type=jnp.float32).astype(jnp.bfloat16).reshape(RESPONSE_ROWS, RESPONSE_LENGTH, KEY_HEADS, group_index, HEAD_DIM)
    critic_pair_rows = jnp.dot(token_rows, critic_key_value.reshape(MODEL_DIM, -1), preferred_element_type=jnp.float32).astype(jnp.bfloat16).reshape(RESPONSE_ROWS, RESPONSE_LENGTH, KEY_HEADS, 2 * HEAD_DIM)
    keys_all = critic_pair_rows[..., :HEAD_DIM].astype(jnp.float32)
    values_all = critic_pair_rows[..., HEAD_DIM:].astype(jnp.float32)
    scores = jnp.einsum('stkgd,sukd->skgtu', critic_query_rows.astype(jnp.float32), keys_all) * scale_factor
    later = lax.broadcasted_iota(jnp.int32, (RESPONSE_LENGTH, RESPONSE_LENGTH), 1)
    earlier = lax.broadcasted_iota(jnp.int32, (RESPONSE_LENGTH, RESPONSE_LENGTH), 0)
    allowed = (later[None] <= earlier[None]) & (later[None] < response_len[:, None, None])
    scores = jnp.where(allowed[:, None, None], scores, -1e30)
    top = jnp.max(scores, -1, keepdims=True)
    expo = jnp.exp(scores - top)
    weights = (expo / jnp.sum(expo, -1, keepdims=True)).astype(jnp.bfloat16).astype(jnp.float32)
    mixed = jnp.einsum('skgtu,sukd->stkgd', weights, values_all).astype(jnp.bfloat16).reshape(RESPONSE_ROWS, RESPONSE_LENGTH, -1)
    token_values = jnp.dot(mixed.astype(jnp.float32), score_weight.astype(jnp.float32))
    valid = lax.broadcasted_iota(jnp.int32, (RESPONSE_ROWS, RESPONSE_LENGTH), 1) < response_len[:, None]
    token_values = jnp.where(valid, token_values, 0.0)

    dest = assign[:, 0].reshape(N_DP, RR)
    onehot = (dest[:, :, None] == jnp.arange(N_DP, dtype=jnp.int32)[None, None, :]).astype(jnp.int32)
    rank = jnp.sum((jnp.cumsum(onehot, 1) - onehot) * onehot, 2)
    block = lax.broadcasted_iota(jnp.int32, (N_DP, RR), 0)
    slot = (block * CAPR + rank).reshape(-1)
    values = jnp.zeros((N_DP, N_DP * CAPR, RESPONSE_LENGTH), jnp.float32).at[dest.reshape(-1), slot].set(token_values)
    return decode_out, values
```

```python
import jax
import jax.numpy as jnp
from jax import lax
from jax.sharding import Mesh, PartitionSpec as P

QUERY_HEADS = 64
KEY_HEADS = 8
HEAD_DIM = 128
STEPS = 2
CAPR = 2
F32 = jnp.float32
BF16 = jnp.bfloat16
SCALE = HEAD_DIM ** (-0.5)


def dot(a, b):
    return jnp.dot(a, b, preferred_element_type=F32)


def swap(x):
    return lax.ppermute(x, "core", [(0, 1), (1, 0)])


def exchange(pieces, axes):
    return lax.all_to_all(pieces, axes, 0, 0, tiled=True)


def add_up(pieces):
    total = pieces[0].astype(F32)
    for i in range(1, pieces.shape[0]):
        total = total + pieces[i].astype(F32)
    return total


def pick(x, index, axis):
    return lax.dynamic_index_in_dim(x, index, axis, keepdims=False)


def cached_attention(q, cache_keys, cache_values, cache_mask, new_keys, new_values):
    old_scores = jnp.einsum("rkgd,rckd->rkgc", q, cache_keys, preferred_element_type=F32) * SCALE
    old_scores = jnp.where(cache_mask[:, None, None, :], old_scores, -1e30)
    new_scores = jnp.einsum("rkgd,trkd->rkgt", q, new_keys, preferred_element_type=F32) * SCALE
    top = jnp.maximum(jnp.max(old_scores, -1), jnp.max(new_scores, -1))
    old_exp = jnp.exp(old_scores - top[..., None])
    new_exp = jnp.exp(new_scores - top[..., None])
    total = jnp.sum(old_exp, -1) + jnp.sum(new_exp, -1)
    old_weights = (old_exp / total[..., None]).astype(BF16)
    new_weights = (new_exp / total[..., None]).astype(BF16)
    mixed = jnp.einsum("rkgc,rckd->rkgd", old_weights, cache_values, preferred_element_type=F32)
    mixed = mixed + jnp.einsum("rkgt,trkd->rkgd", new_weights, new_values, preferred_element_type=F32)
    return mixed.astype(BF16)


def critic_partials(queries, pairs, lengths, score_weight):
    rows, tok_len = queries.shape[:2]
    scores = (
        jnp.einsum("stkgd,sukd->skgtu", queries, pairs[..., :HEAD_DIM], preferred_element_type=F32)
        * SCALE
    )
    later = lax.broadcasted_iota(jnp.int32, (tok_len, tok_len), 1)
    earlier = lax.broadcasted_iota(jnp.int32, (tok_len, tok_len), 0)
    allowed = (later[None] <= earlier[None]) & (later[None] < lengths[:, None, None])
    scores = jnp.where(allowed[:, None, None], scores, -1e30)
    top = jnp.max(scores, -1, keepdims=True)
    expo = jnp.exp(scores - top)
    weights = (expo / jnp.sum(expo, -1, keepdims=True)).astype(BF16)
    mixed = jnp.einsum("skgtu,sukd->stkgd", weights, pairs[..., HEAD_DIM:], preferred_element_type=F32)
    mixed = mixed.astype(BF16).reshape(rows, tok_len, -1)
    partial_values = dot(mixed, score_weight)
    valid = lax.broadcasted_iota(jnp.int32, (rows, tok_len), 1) < lengths[:, None]
    return jnp.where(valid, partial_values, 0.0)


def per_device(
    layer_inputs,
    policy_query_weight,
    policy_key_value,
    policy_out,
    kv_cache,
    prefix_len,
    responses,
    response_len,
    assign,
    critic_query_weight,
    critic_key_value,
    score_weight,
):
    chips = lax.axis_size("chip")
    zs = lax.axis_size("tensor")
    core = lax.axis_index("core")
    shards = chips * 2
    rows = kv_cache.shape[0]
    heads = kv_cache.shape[2]
    group = QUERY_HEADS // KEY_HEADS
    width = policy_query_weight.shape[0]
    q_width = policy_query_weight.shape[1]
    piece = layer_inputs.shape[1]
    half = chips * rows

    src_rows, tok_len, model_width = responses.shape
    tokens = src_rows * tok_len
    split = responses.reshape(tokens, chips, 2, width)
    tok_mine = exchange(pick(split, core, 2).transpose(1, 0, 2), "chip")
    tok_other = exchange(pick(split, 1 - core, 2).transpose(1, 0, 2), "chip")

    pk = policy_key_value.reshape(width, -1)
    wq, wk, wo = (policy_query_weight, swap(policy_query_weight)), (pk, swap(pk)), (policy_out, swap(policy_out))
    cache_keys = kv_cache[..., :HEAD_DIM]
    cache_values = kv_cache[..., HEAD_DIM:]
    cache_mask = lax.broadcasted_iota(jnp.int32, (rows, kv_cache.shape[1]), 1) < prefix_len[:, None]

    by_core = layer_inputs.reshape(chips, 2, rows, piece)
    kept = pick(by_core, core, 1).reshape(half, piece)
    got = swap(pick(by_core, 1 - core, 1).reshape(half, piece))
    state = jnp.concatenate([kept, got], 1)
    fresh = []
    outputs = []
    for step in range(STEPS):
        spread = exchange(jnp.broadcast_to(state[None], (zs, half, 2 * piece)), "tensor")
        spread = spread.reshape(zs, half, 2, piece).transpose(2, 1, 0, 3).reshape(2, half, width)
        q_part = (dot(spread[0], wq[0]) + dot(spread[1], wq[1])).astype(BF16)
        k_part = (dot(spread[0], wk[0]) + dot(spread[1], wk[1])).astype(BF16)
        part = jnp.concatenate([q_part, k_part], 1)
        projected = add_up(exchange(part.reshape(chips, rows, -1), "chip")).astype(BF16)
        q = projected[:, :q_width].reshape(rows, heads, group, HEAD_DIM)
        fresh.append(projected[:, q_width:].reshape(rows, heads, 2 * HEAD_DIM))
        fresh_all = jnp.stack(fresh)
        attended = cached_attention(
            q, cache_keys, cache_values, cache_mask, fresh_all[..., :HEAD_DIM], fresh_all[..., HEAD_DIM:]
        ).reshape(rows, q_width)
        gathered = exchange(jnp.broadcast_to(attended[None], (chips, rows, q_width)), "chip").reshape(half, q_width)
        mine = dot(gathered, wo[0]).astype(BF16).reshape(half, zs, piece)
        other = dot(gathered, wo[1]).astype(BF16).reshape(half, zs, piece)
        term = jnp.concatenate([mine, other], 2).transpose(1, 0, 2)
        summed = add_up(exchange(term, "tensor"))
        state = (state.astype(F32) + summed).astype(BF16)
        back = swap(state[:, piece:]).reshape(chips, 1, rows, piece)
        own = state[:, :piece].reshape(chips, 1, rows, piece)
        both = jnp.where(core == 0, jnp.concatenate([own, back], 1), jnp.concatenate([back, own], 1))
        outputs.append(both.reshape(shards * rows, piece))
    decode_out = jnp.stack(outputs)

    ck = critic_key_value.reshape(width, -1)
    ck_other = swap(ck)
    cq_other = swap(critic_query_weight)
    tm = tok_mine.reshape(chips * tokens, width)
    to = tok_other.reshape(chips * tokens, width)
    kv_part = (dot(tm, ck) + dot(to, ck_other)).astype(BF16)
    q_part = (dot(tm, critic_query_weight) + dot(to, cq_other)).astype(BF16)
    slot_kv = add_up(exchange(kv_part.reshape(chips, tokens, -1), "chip")).astype(BF16)
    slot_q = add_up(exchange(q_part.reshape(chips, tokens, -1), "chip")).astype(BF16)
    partial_values = critic_partials(
        slot_q.reshape(src_rows, tok_len, heads, group, HEAD_DIM),
        slot_kv.reshape(src_rows, tok_len, heads, 2 * HEAD_DIM),
        response_len,
        score_weight,
    )
    dest = assign[:, 0]
    onehot = (dest[:, None] == lax.broadcasted_iota(jnp.int32, (1, shards), 1)).astype(jnp.int32)
    rank = jnp.sum((jnp.cumsum(onehot, 0) - onehot) * onehot, 1)
    slot = dest * CAPR + rank
    chosen = lax.broadcasted_iota(jnp.int32, (shards * CAPR, src_rows), 0) == slot[None, :]
    packed = jnp.sum(jnp.where(chosen[:, :, None], partial_values[None], 0.0), 1)
    packed = jnp.broadcast_to(packed.reshape(shards, 1, CAPR, tok_len), (shards, zs, CAPR, tok_len))
    arrived = exchange(packed.reshape(shards * zs, CAPR, tok_len), ("chip", "core", "tensor"))
    values = jnp.sum(arrived.reshape(shards, zs, CAPR, tok_len), 1)
    return decode_out, values.reshape(1, shards * CAPR, tok_len)


def solution(mesh):
    dp, tensor = mesh.shape["dp"], mesh.shape["tensor"]
    fine = Mesh(mesh.devices.reshape(dp // 2, 2, tensor), ("chip", "core", "tensor"))
    rows = ("chip", "core")
    every = ("chip", "core", "tensor")
    return jax.shard_map(
        per_device,
        mesh=fine,
        in_specs=(
            P(None, every),
            P(rows, "tensor"),
            P(rows, "tensor", None),
            P("tensor", rows),
            P(rows, None, "tensor", None),
            P(rows),
            P(rows, None, None),
            P(rows),
            P(rows, None),
            P(rows, "tensor"),
            P(rows, "tensor", None),
            P("tensor"),
        ),
        out_specs=(P(None, None, every), P(rows, None, None)),
        check_vma=False,
    )
```

```python
import jax
import jax.numpy as jnp
from jax import lax
from jax.experimental import pallas as pl
from jax.experimental.pallas import tpu as pltpu
from jax.sharding import Mesh, PartitionSpec as P

QUERY_HEADS = 64
KEY_HEADS = 8
HEAD_DIM = 128
STEPS = 2
CAPR = 2
F32 = jnp.float32
BF16 = jnp.bfloat16
SCALE = HEAD_DIM ** (-0.5)


def dot(a, b):
    return jnp.dot(a, b, preferred_element_type=F32)


def swap(x):
    return lax.ppermute(x, "core", [(0, 1), (1, 0)])


def flip(x, axes, s, count):
    return lax.ppermute(x, axes, [(i, i ^ s) for i in range(count)])


def exchange(pieces, axes):
    return lax.all_to_all(pieces, axes, 0, 0, tiled=True)


def add_up(pieces):
    total = pieces[0].astype(F32)
    for i in range(1, pieces.shape[0]):
        total = total + pieces[i].astype(F32)
    return total


def pick(x, index, axis):
    return lax.dynamic_index_in_dim(x, index, axis, keepdims=False)


def two_sided(x_mine, x_other, specs, wide, narrow, rows, depth, steps):
    n_wide, n_narrow = wide[0].shape[1], narrow[0].shape[1]

    def kernel(xm, xo, a0, a1, b0, b1, out, acc):
        k = pl.program_id(0)
        left = xm[...].reshape(rows, depth)
        right = xo[...].reshape(rows, depth)
        first = dot(left, a0[...]) + dot(right, a1[...])
        second = dot(left, b0[...]) + dot(right, b1[...])

        @pl.when(k == 0)
        def _():
            acc[:, :n_wide] = first
            acc[:, n_wide:] = second

        @pl.when(k > 0)
        def _():
            acc[:, :n_wide] += first
            acc[:, n_wide:] += second

        @pl.when(k == steps - 1)
        def _():
            out[...] = acc[...].astype(BF16)

    return pl.pallas_call(
        kernel,
        grid=(steps,),
        in_specs=list(specs)
        + [pl.BlockSpec((depth, n_wide), lambda k: (k, 0))] * 2
        + [pl.BlockSpec((depth, n_narrow), lambda k: (k, 0))] * 2,
        out_specs=pl.BlockSpec((rows, n_wide + n_narrow), lambda k: (0, 0)),
        out_shape=jax.ShapeDtypeStruct((rows, n_wide + n_narrow), BF16),
        scratch_shapes=[pltpu.VMEM((rows, n_wide + n_narrow), F32)],
        name="two_sided",
    )(x_mine, x_other, wide[0], wide[1], narrow[0], narrow[1])


def halves_product(x, wide, narrow):
    rows, width = x.shape[0], wide[0].shape[0]
    depth = min(256, width)
    steps = width // depth
    specs = (
        pl.BlockSpec((rows, depth), lambda k: (0, k)),
        pl.BlockSpec((rows, depth), lambda k: (0, steps + k)),
    )
    return two_sided(x, x, specs, wide, narrow, rows, depth, steps)


def pieces_product(x, wide, narrow):
    zs, rows, both = x.shape
    piece = both // 2
    if piece % 128:
        flat = x.reshape(zs, rows, 2, piece).transpose(1, 2, 0, 3).reshape(rows, zs * both)
        return halves_product(flat, wide, narrow)
    specs = (
        pl.BlockSpec((1, rows, piece), lambda k: (k, 0, 0)),
        pl.BlockSpec((1, rows, piece), lambda k: (k, 0, 1)),
    )
    return two_sided(x, x, specs, wide, narrow, rows, piece, zs)


def output_terms(x, weights, zs):
    rows, depth = x.shape
    piece = weights[0].shape[1] // zs
    if piece % 128:
        mine = dot(x, weights[0]).astype(BF16).reshape(rows, zs, piece)
        other = dot(x, weights[1]).astype(BF16).reshape(rows, zs, piece)
        return jnp.concatenate([mine, other], 2).transpose(1, 0, 2)

    def kernel(xr, a, b, out):
        out[0, :, :piece] = dot(xr[...], a[...]).astype(BF16)
        out[0, :, piece:] = dot(xr[...], b[...]).astype(BF16)

    return pl.pallas_call(
        kernel,
        grid=(zs,),
        in_specs=[pl.BlockSpec((rows, depth), lambda t: (0, 0))]
        + [pl.BlockSpec((depth, piece), lambda t: (0, t))] * 2,
        out_specs=pl.BlockSpec((1, rows, 2 * piece), lambda t: (t, 0, 0)),
        out_shape=jax.ShapeDtypeStruct((zs, rows, 2 * piece), BF16),
        name="output_terms",
    )(x, weights[0], weights[1])


def cached_attention(q, cache_keys, cache_values, cache_mask, new_keys, new_values, step):
    old_scores = jnp.einsum("rkgd,rckd->rkgc", q, cache_keys, preferred_element_type=F32) * SCALE
    old_scores = jnp.where(cache_mask[:, None, None, :], old_scores, -1e30)
    new_scores = jnp.einsum("rkgd,trkd->rkgt", q, new_keys, preferred_element_type=F32) * SCALE
    known = lax.broadcasted_iota(jnp.int32, new_scores.shape, 3) <= step
    new_scores = jnp.where(known, new_scores, -1e30)
    top = jnp.maximum(jnp.max(old_scores, -1), jnp.max(new_scores, -1))
    old_exp = jnp.exp(old_scores - top[..., None])
    new_exp = jnp.exp(new_scores - top[..., None])
    total = jnp.sum(old_exp, -1) + jnp.sum(new_exp, -1)
    old_weights = (old_exp / total[..., None]).astype(BF16)
    new_weights = (new_exp / total[..., None]).astype(BF16)
    mixed = jnp.einsum("rkgc,rckd->rkgd", old_weights, cache_values, preferred_element_type=F32)
    mixed = mixed + jnp.einsum("rkgt,trkd->rkgd", new_weights, new_values, preferred_element_type=F32)
    return mixed.astype(BF16)


def critic_partials(queries, pairs, lengths, score_weight):
    rows, tok_len = queries.shape[:2]
    scores = (
        jnp.einsum("stkgd,sukd->skgtu", queries, pairs[..., :HEAD_DIM], preferred_element_type=F32)
        * SCALE
    )
    later = lax.broadcasted_iota(jnp.int32, (tok_len, tok_len), 1)
    earlier = lax.broadcasted_iota(jnp.int32, (tok_len, tok_len), 0)
    allowed = (later[None] <= earlier[None]) & (later[None] < lengths[:, None, None])
    scores = jnp.where(allowed[:, None, None], scores, -1e30)
    top = jnp.max(scores, -1, keepdims=True)
    expo = jnp.exp(scores - top)
    weights = (expo / jnp.sum(expo, -1, keepdims=True)).astype(BF16)
    mixed = jnp.einsum("skgtu,sukd->stkgd", weights, pairs[..., HEAD_DIM:], preferred_element_type=F32)
    mixed = mixed.astype(BF16).reshape(rows, tok_len, -1)
    partial_values = dot(mixed, score_weight)
    valid = lax.broadcasted_iota(jnp.int32, (rows, tok_len), 1) < lengths[:, None]
    return jnp.where(valid, partial_values, 0.0)


def by_flip(x, me):
    n = x.shape[0]
    at = lax.broadcasted_iota(jnp.int32, (n, n), 0) ^ me
    chosen = at == lax.broadcasted_iota(jnp.int32, (n, n), 1)
    return jnp.sum(jnp.where(chosen[:, :, None, None], x[None], 0.0), 1)


def per_device(
    layer_inputs,
    policy_query_weight,
    policy_key_value,
    policy_out,
    kv_cache,
    prefix_len,
    responses,
    response_len,
    assign,
    critic_query_weight,
    critic_key_value,
    score_weight,
):
    chips = lax.axis_size("chip")
    zs = lax.axis_size("tensor")
    core = lax.axis_index("core")
    chip = lax.axis_index("chip")
    odd = lax.axis_index("tensor") & 1
    shards = chips * 2
    rows = kv_cache.shape[0]
    heads = kv_cache.shape[2]
    group = QUERY_HEADS // KEY_HEADS
    width = policy_query_weight.shape[0]
    q_width = policy_query_weight.shape[1]
    piece = layer_inputs.shape[1]
    half = chips * rows
    src_rows, tok_len, model_width = responses.shape
    tokens = src_rows * tok_len
    flat = responses.reshape(tokens, model_width)

    def features(s, part):
        start = (odd ^ part) * (tokens // 2)
        column = (chip ^ s) * (2 * width)
        mine = lax.dynamic_slice(flat, (start, column + core * width), (tokens // 2, width))
        other = lax.dynamic_slice(flat, (start, column + (1 - core) * width), (tokens // 2, width))
        return jnp.concatenate([mine, other], 1)

    def turned(x):
        return jnp.where(odd == 0, x, jnp.roll(x, src_rows // 2, 0))

    pk = policy_key_value.reshape(width, -1)
    ck = critic_key_value.reshape(width, -1)
    by_core = layer_inputs.reshape(chips, 2, rows, piece)
    kept = pick(by_core, core, 1).reshape(half, piece)
    got = swap(pick(by_core, 1 - core, 1).reshape(half, piece))
    state = jnp.concatenate([kept, got], 1)
    wq = (policy_query_weight, swap(policy_query_weight))
    wk = (pk, swap(pk))
    wo = (policy_out, swap(policy_out))
    cq = (critic_query_weight, swap(critic_query_weight))
    ck = (ck, swap(ck))

    near = {s: flip(features(s, 0), "chip", s, chips) for s in range(1, chips)}
    far = {s: flip(near[s], "tensor", 1, zs) for s in near}
    cache_keys = kv_cache[..., :HEAD_DIM]
    cache_values = kv_cache[..., HEAD_DIM:]
    cache_mask = lax.broadcasted_iota(jnp.int32, (rows, kv_cache.shape[1]), 1) < prefix_len[:, None]

    def spread_out(state):
        return exchange(jnp.broadcast_to(state[None], (zs, half, 2 * piece)), "tensor")

    fresh = []

    def attend(projected, step):
        q = projected[:, :q_width].reshape(rows, heads, group, HEAD_DIM)
        fresh.append(projected[:, q_width:].reshape(rows, heads, 2 * HEAD_DIM))
        fresh_all = jnp.stack(fresh + [fresh[0]] * (STEPS - len(fresh)))
        return cached_attention(
            q,
            cache_keys,
            cache_values,
            cache_mask,
            fresh_all[..., :HEAD_DIM],
            fresh_all[..., HEAD_DIM:],
            step,
        ).reshape(rows, q_width)

    def gather_rows(attended):
        copies = jnp.broadcast_to(attended[None], (chips, rows, q_width))
        return exchange(copies, "chip").reshape(half, q_width)

    def own_features(state):
        back = swap(state[:, piece:]).reshape(chips, 1, rows, piece)
        own = state[:, :piece].reshape(chips, 1, rows, piece)
        both = jnp.where(core == 0, jnp.concatenate([own, back], 1), jnp.concatenate([back, own], 1))
        return both.reshape(shards * rows, piece)

    part = pieces_product(spread_out(state), wq, wk)
    arrived = exchange(part.reshape(chips, rows, -1), "chip")
    partials = {0: halves_product(jnp.concatenate([features(0, 0), features(0, 1)], 0), cq, ck)}
    attended = attend(add_up(arrived).astype(BF16), 0)
    gathered = gather_rows(attended)
    ready = {}
    for s in near:
        ready[s] = halves_product(jnp.concatenate([near[s], far[s]], 0), cq, ck)
    for s in near:
        partials[s] = flip(ready[s], "chip", s, chips)
    summed = add_up(exchange(output_terms(gathered, wo, zs), "tensor"))
    state = (state.astype(F32) + summed).astype(BF16)
    spread = spread_out(state)
    outputs = [own_features(state)]
    part = pieces_product(spread, wq, wk)
    arrived = exchange(part.reshape(chips, rows, -1), "chip")
    attended = attend(add_up(arrived).astype(BF16), 1)
    gathered = gather_rows(attended)

    sums = 0.0
    for s in range(chips):
        sums = sums + partials[s].astype(F32)
    sums = sums.astype(BF16)
    partial_values = critic_partials(
        sums[:, :q_width].reshape(src_rows, tok_len, heads, group, HEAD_DIM),
        sums[:, q_width:].reshape(src_rows, tok_len, heads, 2 * HEAD_DIM),
        turned(response_len),
        score_weight,
    )
    dest = assign[:, 0]
    onehot = (dest[:, None] == lax.broadcasted_iota(jnp.int32, (1, shards), 1)).astype(jnp.int32)
    rank = jnp.sum((jnp.cumsum(onehot, 0) - onehot) * onehot, 1)
    slot = turned(dest * CAPR + rank)
    chosen = lax.broadcasted_iota(jnp.int32, (shards * CAPR, src_rows), 0) == slot[None, :]
    packed = jnp.sum(jnp.where(chosen[:, :, None], partial_values[None], 0.0), 1)
    total = packed
    for s in range(1, zs):
        total = total + flip(packed, "tensor", s, zs)
    me = chip * 2 + core
    leaving = by_flip(total.reshape(shards, CAPR, tok_len), me)
    arriving = [leaving[0]]
    for s in range(1, shards):
        arriving.append(flip(leaving[s], ("chip", "core"), s, shards))
    values = by_flip(jnp.stack(arriving), me)

    summed = add_up(exchange(output_terms(gathered, wo, zs), "tensor"))
    state = (state.astype(F32) + summed).astype(BF16)
    outputs.append(own_features(state))
    return jnp.stack(outputs), values.reshape(1, shards * CAPR, tok_len)


def solution(mesh):
    dp, tensor = mesh.shape["dp"], mesh.shape["tensor"]
    fine = Mesh(mesh.devices.reshape(dp // 2, 2, tensor), ("chip", "core", "tensor"))
    rows = ("chip", "core")
    every = ("chip", "core", "tensor")

    return jax.shard_map(
        per_device,
        mesh=fine,
        in_specs=(
            P(None, every),
            P(rows, "tensor"),
            P(rows, "tensor", None),
            P("tensor", rows),
            P(rows, None, "tensor", None),
            P(rows),
            P(rows, None, None),
            P(rows),
            P(rows, None),
            P(rows, "tensor"),
            P(rows, "tensor", None),
            P("tensor"),
        ),
        out_specs=(P(None, None, every), P(rows, None, None)),
        check_vma=False,
    )
```

```python
import jax
import jax.numpy as jnp
from jax import lax
from jax.experimental import pallas as pl
from jax.experimental.pallas import tpu as pltpu
from jax.sharding import Mesh, PartitionSpec as P

QUERY_HEADS = 64
KEY_HEADS = 8
HEAD_DIM = 128
STEPS = 2
CAPR = 2
F32 = jnp.float32
BF16 = jnp.bfloat16
SCALE = HEAD_DIM ** (-0.5)
AHEAD = 2


def dot(a, b):
    return jnp.dot(a, b, preferred_element_type=F32)


def swap(x):
    return lax.ppermute(x, "core", [(0, 1), (1, 0)])


def flip(x, axes, s, count):
    return lax.ppermute(x, axes, [(i, i ^ s) for i in range(count)])


def exchange(pieces, axes):
    return lax.all_to_all(pieces, axes, 0, 0, tiled=True)


def add_up(pieces):
    total = pieces[0].astype(F32)
    for i in range(1, pieces.shape[0]):
        total = total + pieces[i].astype(F32)
    return total


def pick(x, index, axis):
    return lax.dynamic_index_in_dim(x, index, axis, keepdims=False)


def two_sided(place, inputs, moves, moved, wide, narrow, rows, outs):
    width, n_wide = wide[0].shape
    n_narrow = narrow[0].shape[1]
    block = min(512, n_narrow)
    first = n_narrow // block
    steps = first + n_wide // block
    count = len(inputs)
    part = rows // outs

    def kernel(place, *refs):
        xs, weights, results = refs[:count], refs[count : count + 4], refs[count + 4 : count + 4 + outs]
        x, held, x_sems, w_sems = refs[count + 4 + outs :]
        j = pl.program_id(0)

        def weight_copy(i, side):
            source = weights[2 + side] if i < first else weights[side]
            at = i if i < first else i - first
            return pltpu.make_async_copy(
                source.at[:, pl.ds(at * block, block)], held.at[i, side], w_sems.at[i, side]
            )

        @pl.when(j == 0)
        def _():
            copies = [
                pltpu.make_async_copy(source, target, x_sems.at[i])
                for i, (source, target) in enumerate(moves(place, xs, x))
            ]
            for copy in copies:
                copy.start()
            for i in range(min(AHEAD, steps)):
                for side in range(2):
                    weight_copy(i, side).start()
            for copy in copies:
                copy.wait()

        for i in range(steps):

            @pl.when(j == i)
            def _(i=i):
                if i + AHEAD < steps:
                    for side in range(2):
                        weight_copy(i + AHEAD, side).start()
                weight_copy(i, 0).wait()
                weight_copy(i, 1).wait()
                total = dot(x[:, :width], held[i, 0]) + dot(x[:, width:], held[i, 1])
                for k, result in enumerate(results):
                    result[...] = total[k * part : (k + 1) * part].astype(BF16)

    return pl.pallas_call(
        kernel,
        grid_spec=pltpu.PrefetchScalarGridSpec(
            num_scalar_prefetch=1,
            grid=(steps,),
            in_specs=[pl.BlockSpec(memory_space=pl.ANY)] * (count + 4),
            out_specs=[
                pl.BlockSpec((part, block), lambda j, place: (0, jnp.where(j < first, j + n_wide // block, j - first)))
                for _ in range(outs)
            ],
            scratch_shapes=[
                pltpu.VMEM((rows, 2 * width), BF16),
                pltpu.VMEM((steps, 2, width, block), BF16),
                pltpu.SemaphoreType.DMA((moved,)),
                pltpu.SemaphoreType.DMA((steps, 2)),
            ],
        ),
        out_shape=[jax.ShapeDtypeStruct((part, n_wide + n_narrow), BF16) for _ in range(outs)],
        name="two_sided",
    )(place, *inputs, wide[0], wide[1], narrow[0], narrow[1])


def blocks_product(place, blocks, tokens, wide, narrow):
    width = wide[0].shape[0]
    part = tokens // 2
    inputs = [x for block in blocks for x in block]

    def moves(place, xs, x):
        core, odd, chip = place[0], place[1], place[2]
        refs = iter(xs)
        row = 0
        for block in blocks:
            own = [next(refs) for _ in block]
            for i in range(2):
                ref = own[i] if len(own) == 2 else own[0]
                start = 0 if len(own) == 2 else pl.multiple_of((odd ^ i) * part, part)
                base = chip * (2 * width) if ref.shape[1] > 2 * width else 0
                for side, column in enumerate((core, 1 - core)):
                    at = pl.multiple_of(base + column * width, 128)
                    yield (
                        ref.at[pl.ds(start, part), pl.ds(at, width)],
                        x.at[pl.ds(row, part), pl.ds(side * width, width)],
                    )
                row += part

    count = len(blocks)
    return two_sided(place, inputs, moves, 4 * count, wide, narrow, tokens * count, count)


def pieces_product(place, x, wide, narrow):
    zs, rows, both = x.shape
    piece = both // 2
    width = zs * piece
    if piece % 128:
        x = x.reshape(zs, rows, 2, piece).transpose(2, 1, 0, 3).reshape(2, rows, width)

    def moves(place, xs, x):
        for t in range(xs[0].shape[0]):
            for side in range(2):
                if piece % 128:
                    if t == side:
                        yield xs[0].at[t], x.at[:, pl.ds(side * width, width)]
                else:
                    source = xs[0].at[t, :, pl.ds(side * piece, piece)]
                    yield source, x.at[:, pl.ds(side * width + t * piece, piece)]

    moved = 2 if piece % 128 else 2 * zs
    return two_sided(place, [x], moves, moved, wide, narrow, rows, 1)[0]


def output_terms(x, weights, zs):
    rows, depth = x.shape
    piece = weights[0].shape[1] // zs
    if piece % 128:
        mine = dot(x, weights[0]).astype(BF16).reshape(rows, zs, piece)
        other = dot(x, weights[1]).astype(BF16).reshape(rows, zs, piece)
        return jnp.concatenate([mine, other], 2).transpose(1, 0, 2)

    def kernel(source, a, b, out, x, held, x_sem, w_sems):
        j = pl.program_id(0)

        def weight_copy(i, side):
            return pltpu.make_async_copy(
                (a, b)[side].at[:, pl.ds(i * piece, piece)], held.at[i, side], w_sems.at[i, side]
            )

        @pl.when(j == 0)
        def _():
            copy = pltpu.make_async_copy(source, x, x_sem)
            copy.start()
            for i in range(min(AHEAD, zs)):
                for side in range(2):
                    weight_copy(i, side).start()
            copy.wait()

        for i in range(zs):

            @pl.when(j == i)
            def _(i=i):
                if i + AHEAD < zs:
                    for side in range(2):
                        weight_copy(i + AHEAD, side).start()
                for side in range(2):
                    weight_copy(i, side).wait()
                    out[0, :, side * piece : (side + 1) * piece] = dot(x[...], held[i, side]).astype(BF16)

    return pl.pallas_call(
        kernel,
        grid=(zs,),
        in_specs=[pl.BlockSpec(memory_space=pl.ANY)] * 3,
        out_specs=pl.BlockSpec((1, rows, 2 * piece), lambda t: (t, 0, 0)),
        out_shape=jax.ShapeDtypeStruct((zs, rows, 2 * piece), BF16),
        scratch_shapes=[
            pltpu.VMEM((rows, depth), BF16),
            pltpu.VMEM((zs, 2, depth, piece), BF16),
            pltpu.SemaphoreType.DMA,
            pltpu.SemaphoreType.DMA((zs, 2)),
        ],
        name="output_terms",
    )(x, weights[0], weights[1])


def cached_attention(q, cache_keys, cache_values, cache_mask, new_keys, new_values, step):
    old_scores = jnp.einsum("rkgd,rckd->rkgc", q, cache_keys, preferred_element_type=F32) * SCALE
    old_scores = jnp.where(cache_mask[:, None, None, :], old_scores, -1e30)
    new_scores = jnp.einsum("rkgd,trkd->rkgt", q, new_keys, preferred_element_type=F32) * SCALE
    known = lax.broadcasted_iota(jnp.int32, new_scores.shape, 3) <= step
    new_scores = jnp.where(known, new_scores, -1e30)
    top = jnp.maximum(jnp.max(old_scores, -1), jnp.max(new_scores, -1))
    old_exp = jnp.exp(old_scores - top[..., None])
    new_exp = jnp.exp(new_scores - top[..., None])
    total = jnp.sum(old_exp, -1) + jnp.sum(new_exp, -1)
    old_weights = (old_exp / total[..., None]).astype(BF16)
    new_weights = (new_exp / total[..., None]).astype(BF16)
    mixed = jnp.einsum("rkgc,rckd->rkgd", old_weights, cache_values, preferred_element_type=F32)
    mixed = mixed + jnp.einsum("rkgt,trkd->rkgd", new_weights, new_values, preferred_element_type=F32)
    return mixed.astype(BF16)


def critic_partials(parts, last, score_weight, tok_len, heads, group):
    tokens, columns = parts[0].shape
    part = tokens // 2
    q_width = heads * group * HEAD_DIM

    def kernel(*refs):
        xs, last_ref, weight, out = refs[:-3], refs[-3], refs[-2], refs[-1]

        def total(start, size):
            at = slice(start, start + size)
            x = xs[0][:, at].astype(F32)
            for ref in xs[1:]:
                x = x + ref[:, at].astype(F32)
            return x.astype(BF16)

        row = lax.broadcasted_iota(jnp.int32, (part, part), 0)
        column = lax.broadcasted_iota(jnp.int32, (part, part), 1)
        allowed = (column >= row - row % tok_len) & (column <= last_ref[...])
        bias = jnp.where(allowed, 0.0, -1e30)
        bias = jnp.concatenate([bias] * group, 0)
        share = jnp.zeros((part, HEAD_DIM), F32)
        for head in range(heads):
            pair = total(q_width + head * 2 * HEAD_DIM, 2 * HEAD_DIM)
            start = head * group * HEAD_DIM
            wide = total(start, group * HEAD_DIM)
            queries = jnp.concatenate([wide[:, g * HEAD_DIM : (g + 1) * HEAD_DIM] for g in range(group)], 0)
            scores = SCALE * lax.dot_general(
                queries, pair[:, :HEAD_DIM], (((1,), (1,)), ((), ())), preferred_element_type=F32
            )
            scores = jnp.where(bias < 0.0, -1e30, scores)
            expo = jnp.exp(scores - jnp.max(scores, -1, keepdims=True))
            weights = (expo * (1.0 / jnp.sum(expo, -1, keepdims=True))).astype(BF16)
            mixed = dot(weights, pair[:, HEAD_DIM:]).astype(BF16).astype(F32)
            for g in range(group):
                at = slice(start + g * HEAD_DIM, start + (g + 1) * HEAD_DIM)
                share = share + mixed[g * part : (g + 1) * part] * weight[:, at].astype(F32)
        out[...] = jnp.sum(share.reshape(part // tok_len, tok_len, HEAD_DIM), -1)

    return pl.pallas_call(
        kernel,
        grid=(2,),
        in_specs=[pl.BlockSpec((part, columns), lambda i: (i, 0))] * len(parts)
        + [pl.BlockSpec((part, 1), lambda i: (i, 0)), pl.BlockSpec((1, q_width), lambda i: (0, 0))],
        out_specs=pl.BlockSpec((part // tok_len, tok_len), lambda i: (i, 0)),
        out_shape=jax.ShapeDtypeStruct((tokens // tok_len, tok_len), F32),
        name="critic_partials",
    )(*parts, last, score_weight.reshape(1, q_width))


def by_flip(x, me):
    n = x.shape[0]
    at = lax.broadcasted_iota(jnp.int32, (n, n), 0) ^ me
    chosen = at == lax.broadcasted_iota(jnp.int32, (n, n), 1)
    return jnp.sum(jnp.where(chosen.reshape((n, n) + (1,) * (x.ndim - 1)), x[None], 0.0), 1)


def per_device(
    layer_inputs,
    policy_query_weight,
    policy_key_value,
    policy_out,
    kv_cache,
    prefix_len,
    responses,
    response_len,
    assign,
    critic_query_weight,
    critic_key_value,
    score_weight,
):
    chips = lax.axis_size("chip")
    zs = lax.axis_size("tensor")
    core = lax.axis_index("core")
    chip = lax.axis_index("chip")
    odd = lax.axis_index("tensor") & 1
    shards = chips * 2
    rows = kv_cache.shape[0]
    heads = kv_cache.shape[2]
    group = QUERY_HEADS // KEY_HEADS
    width = policy_query_weight.shape[0]
    q_width = policy_query_weight.shape[1]
    piece = layer_inputs.shape[1]
    half = chips * rows
    src_rows, tok_len, model_width = responses.shape
    tokens = src_rows * tok_len
    flat = responses.reshape(tokens, model_width)

    place = jnp.stack([core, odd, chip]).astype(jnp.int32)

    def features(s, start, count):
        return lax.dynamic_slice(flat, (start, (chip ^ s) * (2 * width)), (count, 2 * width))

    def turned(x):
        return jnp.where(odd == 0, x, jnp.roll(x, src_rows // 2, 0))

    pk = policy_key_value.reshape(width, -1)
    ck = critic_key_value.reshape(width, -1)
    by_core = layer_inputs.reshape(chips, 2, rows, piece)
    kept = pick(by_core, core, 1).reshape(half, piece)
    got = swap(pick(by_core, 1 - core, 1).reshape(half, piece))
    state = jnp.concatenate([kept, got], 1)
    wq = (policy_query_weight, swap(policy_query_weight))
    wk = (pk, swap(pk))
    wo = (policy_out, swap(policy_out))
    cq = (critic_query_weight, swap(critic_query_weight))
    ck = (ck, swap(ck))

    early = [s for s in range(1, chips) if 3 * s <= 2 * (chips - 1)]
    late = [s for s in range(1, chips) if s not in early]
    leaving = {s: features(s, odd * (tokens // 2), tokens // 2) for s in range(1, chips)}
    near = {s: flip(leaving[s], "chip", s, chips) for s in leaving}
    far = {s: flip(near[s], "tensor", 1, zs) for s in near}
    cache_keys = kv_cache[..., :HEAD_DIM]
    cache_values = kv_cache[..., HEAD_DIM:]
    cache_mask = lax.broadcasted_iota(jnp.int32, (rows, kv_cache.shape[1]), 1) < prefix_len[:, None]

    def spread_out(state):
        return exchange(jnp.broadcast_to(state[None], (zs, half, 2 * piece)), "tensor")

    fresh = []

    def attend(projected, step):
        q = projected[:, :q_width].reshape(rows, heads, group, HEAD_DIM)
        fresh.append(projected[:, q_width:].reshape(rows, heads, 2 * HEAD_DIM))
        fresh_all = jnp.stack(fresh + [fresh[0]] * (STEPS - len(fresh)))
        return cached_attention(
            q,
            cache_keys,
            cache_values,
            cache_mask,
            fresh_all[..., :HEAD_DIM],
            fresh_all[..., HEAD_DIM:],
            step,
        ).reshape(rows, q_width)

    def gather_rows(attended):
        copies = jnp.broadcast_to(attended[None], (chips, rows, q_width))
        return exchange(copies, "chip").reshape(half, q_width)

    def own_features(state):
        back = swap(state[:, piece:]).reshape(chips, 1, rows, piece)
        own = state[:, :piece].reshape(chips, 1, rows, piece)
        both = jnp.where(core == 0, jnp.concatenate([own, back], 1), jnp.concatenate([back, own], 1))
        return both.reshape(shards * rows, piece)

    spread = spread_out(state)
    part = pieces_product(place, spread, wq, wk)
    arrived = exchange(part.reshape(chips, rows, -1), "chip")
    partials = {0: blocks_product(place, [[flat]], tokens, cq, ck)[0]}
    attended = attend(add_up(arrived).astype(BF16), 0)
    gathered = gather_rows(attended)
    for some in (early, late):
        blocks = [[near[s], far[s]] if s in far else [near[s]] for s in some]
        ready = blocks_product(place, blocks, tokens, cq, ck)
        for s, product in zip(some, ready):
            partials[s] = flip(product, "chip", s, chips)
    summed = add_up(exchange(output_terms(gathered, wo, zs), "tensor"))
    state = (state.astype(F32) + summed).astype(BF16)
    spread = spread_out(state)
    outputs = [own_features(state)]
    part = pieces_product(place, spread, wq, wk)
    arrived = exchange(part.reshape(chips, rows, -1), "chip")
    attended = attend(add_up(arrived).astype(BF16), 1)
    gathered = gather_rows(attended)

    lengths = turned(response_len)
    dest = assign[:, 0]
    onehot = (dest[:, None] == lax.broadcasted_iota(jnp.int32, (1, shards), 1)).astype(jnp.int32)
    rank = jnp.sum((jnp.cumsum(onehot, 0) - onehot) * onehot, 1)
    slot = turned(dest * CAPR + rank)
    chosen = lax.broadcasted_iota(jnp.int32, (shards * CAPR, src_rows), 0) == slot[None, :]
    position = lax.broadcasted_iota(jnp.int32, (src_rows, tok_len), 1)
    valid = position < lengths[:, None]
    base = lax.broadcasted_iota(jnp.int32, (src_rows, tok_len), 0) % (src_rows // 2) * tok_len
    last = (base + jnp.minimum(position, lengths[:, None] - 1)).reshape(tokens, 1)
    kept_here = chosen[:, :, None] & valid[None]
    shares = critic_partials(
        [partials[s] for s in range(chips)], last, score_weight, tok_len, heads, group
    )
    packed = jnp.sum(jnp.where(kept_here, shares[None], 0.0), 1)
    total = packed
    for s in range(1, zs):
        total = total + flip(packed, "tensor", s, zs)
    total = total.reshape(chips, 2, CAPR, tok_len)
    here = pick(total, core, 1)
    there = flip(pick(total, 1 - core, 1), "core", 1, 2)
    both = jnp.where(core == 0, jnp.stack([here, there], 1), jnp.stack([there, here], 1))
    leaving = by_flip(both, chip)
    arriving = [leaving[0]]
    for s in range(1, chips):
        arriving.append(flip(leaving[s], "chip", s, chips))
    values = by_flip(jnp.stack(arriving), chip)

    summed = add_up(exchange(output_terms(gathered, wo, zs), "tensor"))
    state = (state.astype(F32) + summed).astype(BF16)
    outputs.append(own_features(state))
    return jnp.stack(outputs), values.reshape(1, shards * CAPR, tok_len)


def solution(mesh):
    dp, tensor = mesh.shape["dp"], mesh.shape["tensor"]
    fine = Mesh(mesh.devices.reshape(dp // 2, 2, tensor), ("chip", "core", "tensor"))
    rows = ("chip", "core")
    every = ("chip", "core", "tensor")

    return jax.shard_map(
        per_device,
        mesh=fine,
        in_specs=(
            P(None, every),
            P(rows, "tensor"),
            P(rows, "tensor", None),
            P("tensor", rows),
            P(rows, None, "tensor", None),
            P(rows),
            P(rows, None, None),
            P(rows),
            P(rows, None),
            P(rows, "tensor"),
            P(rows, "tensor", None),
            P("tensor"),
        ),
        out_specs=(P(None, None, every), P(rows, None, None)),
        check_vma=False,
    )
```

```python
import jax
import jax.numpy as jnp
from jax import lax
from jax.experimental import pallas as pl
from jax.experimental.pallas import tpu as pltpu
from jax.sharding import Mesh, PartitionSpec as P

QUERY_HEADS = 64
KEY_HEADS = 8
HEAD_DIM = 128
STEPS = 2
CAPR = 2
F32 = jnp.float32
BF16 = jnp.bfloat16
SCALE = HEAD_DIM ** (-0.5)
AHEAD = 2


def dot(a, b):
    return jnp.dot(a, b, preferred_element_type=F32)


def swap(x):
    return lax.ppermute(x, "core", [(0, 1), (1, 0)])


def flip(x, axes, s, count):
    return lax.ppermute(x, axes, [(i, i ^ s) for i in range(count)])


def exchange(pieces, axes):
    return lax.all_to_all(pieces, axes, 0, 0, tiled=True)


def add_up(pieces):
    total = pieces[0].astype(F32)
    for i in range(1, pieces.shape[0]):
        total = total + pieces[i].astype(F32)
    return total


def pick(x, index, axis):
    return lax.dynamic_index_in_dim(x, index, axis, keepdims=False)


def two_sided(place, inputs, moves, moved, wide, narrow, rows, outs, space=pl.ANY):
    width, n_wide = wide[0].shape
    n_narrow = narrow[0].shape[1]
    block = min(512, n_narrow)
    first = n_narrow // block
    steps = first + n_wide // block
    count = len(inputs)
    part = rows // outs

    def kernel(place, *refs):
        xs, weights, results = refs[:count], refs[count : count + 4], refs[count + 4 : count + 4 + outs]
        x, held, x_sems, w_sems = refs[count + 4 + outs :]
        j = pl.program_id(0)

        def weight_copy(i, side):
            source = weights[2 + side] if i < first else weights[side]
            at = i if i < first else i - first
            return pltpu.make_async_copy(
                source.at[:, pl.ds(at * block, block)], held.at[i, side], w_sems.at[i, side]
            )

        @pl.when(j == 0)
        def _():
            copies = [
                pltpu.make_async_copy(source, target, x_sems.at[i])
                for i, (source, target) in enumerate(moves(place, xs, x))
            ]
            for copy in copies:
                copy.start()
            for i in range(min(AHEAD, steps)):
                for side in range(2):
                    weight_copy(i, side).start()
            for copy in copies:
                copy.wait()

        for i in range(steps):

            @pl.when(j == i)
            def _(i=i):
                if i + AHEAD < steps:
                    for side in range(2):
                        weight_copy(i + AHEAD, side).start()
                weight_copy(i, 0).wait()
                weight_copy(i, 1).wait()
                total = dot(x[:, :width], held[i, 0]) + dot(x[:, width:], held[i, 1])
                for k, result in enumerate(results):
                    result[...] = total[k * part : (k + 1) * part].astype(BF16)

    return pl.pallas_call(
        kernel,
        grid_spec=pltpu.PrefetchScalarGridSpec(
            num_scalar_prefetch=1,
            grid=(steps,),
            in_specs=[pl.BlockSpec(memory_space=space)] * count + [pl.BlockSpec(memory_space=pl.ANY)] * 4,
            out_specs=[
                pl.BlockSpec((part, block), lambda j, place: (0, jnp.where(j < first, j + n_wide // block, j - first)))
                for _ in range(outs)
            ],
            scratch_shapes=[
                pltpu.VMEM((rows, 2 * width), BF16),
                pltpu.VMEM((steps, 2, width, block), BF16),
                pltpu.SemaphoreType.DMA((moved,)),
                pltpu.SemaphoreType.DMA((steps, 2)),
            ],
        ),
        out_shape=[jax.ShapeDtypeStruct((part, n_wide + n_narrow), BF16) for _ in range(outs)],
        name="two_sided",
    )(place, *inputs, wide[0], wide[1], narrow[0], narrow[1])


def blocks_product(place, blocks, tokens, wide, narrow):
    width = wide[0].shape[0]
    part = tokens // 2
    inputs = [x for block in blocks for x in block]

    def moves(place, xs, x):
        core, odd, chip = place[0], place[1], place[2]
        refs = iter(xs)
        row = 0
        for block in blocks:
            own = [next(refs) for _ in block]
            for i in range(2):
                ref = own[i] if len(own) == 2 else own[0]
                start = 0 if len(own) == 2 else pl.multiple_of((odd ^ i) * part, part)
                base = chip * (2 * width) if ref.shape[1] > 2 * width else 0
                for side, column in enumerate((core, 1 - core)):
                    at = pl.multiple_of(base + column * width, 128)
                    yield (
                        ref.at[pl.ds(start, part), pl.ds(at, width)],
                        x.at[pl.ds(row, part), pl.ds(side * width, width)],
                    )
                row += part

    count = len(blocks)
    return two_sided(place, inputs, moves, 4 * count, wide, narrow, tokens * count, count)


def pieces_product(place, x, wide, narrow):
    zs, rows, both = x.shape
    piece = both // 2
    width = zs * piece
    if piece % 128:
        x = x.reshape(zs, rows, 2, piece).transpose(2, 1, 0, 3).reshape(2, rows, width)

    def moves(place, xs, x):
        for t in range(xs[0].shape[0]):
            for side in range(2):
                if piece % 128:
                    if t == side:
                        yield xs[0].at[t], x.at[:, pl.ds(side * width, width)]
                else:
                    source = xs[0].at[t, :, pl.ds(side * piece, piece)]
                    yield source, x.at[:, pl.ds(side * width + t * piece, piece)]

    moved = 2 if piece % 128 else 2 * zs
    return two_sided(place, [x], moves, moved, wide, narrow, rows, 1, pltpu.VMEM)[0]


def output_terms(x, weights, zs):
    rows, depth = x.shape
    piece = weights[0].shape[1] // zs
    if piece % 128:
        mine = dot(x, weights[0]).astype(BF16).reshape(rows, zs, piece)
        other = dot(x, weights[1]).astype(BF16).reshape(rows, zs, piece)
        return jnp.concatenate([mine, other], 2).transpose(1, 0, 2)

    def kernel(x, a, b, out, held, w_sems):
        j = pl.program_id(0)

        def weight_copy(i, side):
            return pltpu.make_async_copy(
                (a, b)[side].at[:, pl.ds(i * piece, piece)], held.at[i, side], w_sems.at[i, side]
            )

        @pl.when(j == 0)
        def _():
            for i in range(min(AHEAD, zs)):
                for side in range(2):
                    weight_copy(i, side).start()

        for i in range(zs):

            @pl.when(j == i)
            def _(i=i):
                if i + AHEAD < zs:
                    for side in range(2):
                        weight_copy(i + AHEAD, side).start()
                for side in range(2):
                    weight_copy(i, side).wait()
                    out[0, :, side * piece : (side + 1) * piece] = dot(x[...], held[i, side]).astype(BF16)

    return pl.pallas_call(
        kernel,
        grid=(zs,),
        in_specs=[pl.BlockSpec(memory_space=pltpu.VMEM)] + [pl.BlockSpec(memory_space=pl.ANY)] * 2,
        out_specs=pl.BlockSpec((1, rows, 2 * piece), lambda t: (t, 0, 0)),
        out_shape=jax.ShapeDtypeStruct((zs, rows, 2 * piece), BF16),
        scratch_shapes=[
            pltpu.VMEM((zs, 2, depth, piece), BF16),
            pltpu.SemaphoreType.DMA((zs, 2)),
        ],
        name="output_terms",
    )(x, weights[0], weights[1])


def cached_attention(q, cache_keys, cache_values, cache_mask, new_keys, new_values, step):
    old_scores = jnp.einsum("rkgd,rckd->rkgc", q, cache_keys, preferred_element_type=F32) * SCALE
    old_scores = jnp.where(cache_mask[:, None, None, :], old_scores, -1e30)
    new_scores = jnp.einsum("rkgd,trkd->rkgt", q, new_keys, preferred_element_type=F32) * SCALE
    known = lax.broadcasted_iota(jnp.int32, new_scores.shape, 3) <= step
    new_scores = jnp.where(known, new_scores, -1e30)
    top = jnp.maximum(jnp.max(old_scores, -1), jnp.max(new_scores, -1))
    old_exp = jnp.exp(old_scores - top[..., None])
    new_exp = jnp.exp(new_scores - top[..., None])
    total = jnp.sum(old_exp, -1) + jnp.sum(new_exp, -1)
    old_weights = (old_exp / total[..., None]).astype(BF16)
    new_weights = (new_exp / total[..., None]).astype(BF16)
    mixed = jnp.einsum("rkgc,rckd->rkgd", old_weights, cache_values, preferred_element_type=F32)
    mixed = mixed + jnp.einsum("rkgt,trkd->rkgd", new_weights, new_values, preferred_element_type=F32)
    return mixed.astype(BF16)


def critic_partials(parts, last, score_weight, tok_len, heads, group):
    tokens, columns = parts[0].shape
    part = tokens // 2
    q_width = heads * group * HEAD_DIM

    def kernel(*refs):
        xs, last_ref, weight, out = refs[:-3], refs[-3], refs[-2], refs[-1]

        def total(start, size):
            at = slice(start, start + size)
            x = xs[0][:, at].astype(F32)
            for ref in xs[1:]:
                x = x + ref[:, at].astype(F32)
            return x.astype(BF16)

        row = lax.broadcasted_iota(jnp.int32, (part, part), 0)
        column = lax.broadcasted_iota(jnp.int32, (part, part), 1)
        allowed = (column >= row - row % tok_len) & (column <= last_ref[...])
        bias = jnp.where(allowed, 0.0, -1e30)
        bias = jnp.concatenate([bias] * group, 0)
        share = jnp.zeros((part, HEAD_DIM), F32)
        for head in range(heads):
            pair = total(q_width + head * 2 * HEAD_DIM, 2 * HEAD_DIM)
            start = head * group * HEAD_DIM
            wide = total(start, group * HEAD_DIM)
            queries = jnp.concatenate([wide[:, g * HEAD_DIM : (g + 1) * HEAD_DIM] for g in range(group)], 0)
            scores = SCALE * lax.dot_general(
                queries, pair[:, :HEAD_DIM], (((1,), (1,)), ((), ())), preferred_element_type=F32
            )
            scores = jnp.where(bias < 0.0, -1e30, scores)
            expo = jnp.exp(scores - jnp.max(scores, -1, keepdims=True))
            weights = (expo * (1.0 / jnp.sum(expo, -1, keepdims=True))).astype(BF16)
            mixed = dot(weights, pair[:, HEAD_DIM:]).astype(BF16).astype(F32)
            for g in range(group):
                at = slice(start + g * HEAD_DIM, start + (g + 1) * HEAD_DIM)
                share = share + mixed[g * part : (g + 1) * part] * weight[:, at].astype(F32)
        out[...] = jnp.sum(share.reshape(part // tok_len, tok_len, HEAD_DIM), -1)

    return pl.pallas_call(
        kernel,
        grid=(2,),
        in_specs=[pl.BlockSpec((part, columns), lambda i: (i, 0))] * len(parts)
        + [pl.BlockSpec((part, 1), lambda i: (i, 0)), pl.BlockSpec((1, q_width), lambda i: (0, 0))],
        out_specs=pl.BlockSpec((part // tok_len, tok_len), lambda i: (i, 0)),
        out_shape=jax.ShapeDtypeStruct((tokens // tok_len, tok_len), F32),
        name="critic_partials",
    )(*parts, last, score_weight.reshape(1, q_width))


def by_flip(x, me):
    n = x.shape[0]
    at = lax.broadcasted_iota(jnp.int32, (n, n), 0) ^ me
    chosen = at == lax.broadcasted_iota(jnp.int32, (n, n), 1)
    return jnp.sum(jnp.where(chosen.reshape((n, n) + (1,) * (x.ndim - 1)), x[None], 0.0), 1)


def per_device(
    layer_inputs,
    policy_query_weight,
    policy_key_value,
    policy_out,
    kv_cache,
    prefix_len,
    responses,
    response_len,
    assign,
    critic_query_weight,
    critic_key_value,
    score_weight,
):
    chips = lax.axis_size("chip")
    zs = lax.axis_size("tensor")
    core = lax.axis_index("core")
    chip = lax.axis_index("chip")
    odd = lax.axis_index("tensor") & 1
    shards = chips * 2
    rows = kv_cache.shape[0]
    heads = kv_cache.shape[2]
    group = QUERY_HEADS // KEY_HEADS
    width = policy_query_weight.shape[0]
    q_width = policy_query_weight.shape[1]
    piece = layer_inputs.shape[1]
    half = chips * rows
    src_rows, tok_len, model_width = responses.shape
    tokens = src_rows * tok_len
    flat = responses.reshape(tokens, model_width)

    place = jnp.stack([core, odd, chip]).astype(jnp.int32)

    def features(s, start, count):
        return lax.dynamic_slice(flat, (start, (chip ^ s) * (2 * width)), (count, 2 * width))

    def turned(x):
        return jnp.where(odd == 0, x, jnp.roll(x, src_rows // 2, 0))

    pk = policy_key_value.reshape(width, -1)
    ck = critic_key_value.reshape(width, -1)
    by_core = layer_inputs.reshape(chips, 2, rows, piece)
    kept = pick(by_core, core, 1).reshape(half, piece)
    got = swap(pick(by_core, 1 - core, 1).reshape(half, piece))
    state = jnp.concatenate([kept, got], 1)
    wq = (policy_query_weight, swap(policy_query_weight))
    wk = (pk, swap(pk))
    wo = (policy_out, swap(policy_out))
    cq = (critic_query_weight, swap(critic_query_weight))
    ck = (ck, swap(ck))

    early = [s for s in range(2, chips) if 3 * s <= 2 * (chips - 1)]
    late = [s for s in range(2, chips) if s not in early]
    near = {1: flip(features(1, 0, tokens), "chip", 1, chips)}
    for s in early + late:
        leaving = features(s, odd * (tokens // 2), tokens // 2)
        near[s] = flip(leaving, "chip", s, chips)
    far = {s: flip(near[s], "tensor", 1, zs) for s in early + late}
    cache_keys = kv_cache[..., :HEAD_DIM]
    cache_values = kv_cache[..., HEAD_DIM:]
    cache_mask = lax.broadcasted_iota(jnp.int32, (rows, kv_cache.shape[1]), 1) < prefix_len[:, None]

    def spread_out(state):
        return exchange(jnp.broadcast_to(state[None], (zs, half, 2 * piece)), "tensor")

    fresh = []

    def attend(projected, step):
        q = projected[:, :q_width].reshape(rows, heads, group, HEAD_DIM)
        fresh.append(projected[:, q_width:].reshape(rows, heads, 2 * HEAD_DIM))
        fresh_all = jnp.stack(fresh + [fresh[0]] * (STEPS - len(fresh)))
        return cached_attention(
            q,
            cache_keys,
            cache_values,
            cache_mask,
            fresh_all[..., :HEAD_DIM],
            fresh_all[..., HEAD_DIM:],
            step,
        ).reshape(rows, q_width)

    def gather_rows(attended):
        copies = jnp.broadcast_to(attended[None], (chips, rows, q_width))
        return exchange(copies, "chip").reshape(half, q_width)

    def own_features(state):
        back = swap(state[:, piece:]).reshape(chips, 1, rows, piece)
        own = state[:, :piece].reshape(chips, 1, rows, piece)
        both = jnp.where(core == 0, jnp.concatenate([own, back], 1), jnp.concatenate([back, own], 1))
        return both.reshape(shards * rows, piece)

    spread = spread_out(state)
    part = pieces_product(place, spread, wq, wk)
    arrived = exchange(part.reshape(chips, rows, -1), "chip")
    partials = {0: blocks_product(place, [[flat]], tokens, cq, ck)[0]}
    attended = attend(add_up(arrived).astype(BF16), 0)
    gathered = gather_rows(attended)
    for some in ([1], early, late):
        blocks = [[near[s], far[s]] if s in far else [near[s]] for s in some]
        ready = blocks_product(place, blocks, tokens, cq, ck)
        for s, product in zip(some, ready):
            partials[s] = flip(product, "chip", s, chips)
    summed = add_up(exchange(output_terms(gathered, wo, zs), "tensor"))
    state = (state.astype(F32) + summed).astype(BF16)
    spread = spread_out(state)
    outputs = [own_features(state)]
    part = pieces_product(place, spread, wq, wk)
    arrived = exchange(part.reshape(chips, rows, -1), "chip")
    attended = attend(add_up(arrived).astype(BF16), 1)
    gathered = gather_rows(attended)

    lengths = turned(response_len)
    dest = assign[:, 0]
    onehot = (dest[:, None] == lax.broadcasted_iota(jnp.int32, (1, shards), 1)).astype(jnp.int32)
    rank = jnp.sum((jnp.cumsum(onehot, 0) - onehot) * onehot, 1)
    slot = turned(dest * CAPR + rank)
    chosen = lax.broadcasted_iota(jnp.int32, (shards * CAPR, src_rows), 0) == slot[None, :]
    position = lax.broadcasted_iota(jnp.int32, (src_rows, tok_len), 1)
    valid = position < lengths[:, None]
    base = lax.broadcasted_iota(jnp.int32, (src_rows, tok_len), 0) % (src_rows // 2) * tok_len
    last = (base + jnp.minimum(position, lengths[:, None] - 1)).reshape(tokens, 1)
    kept_here = chosen[:, :, None] & valid[None]
    shares = critic_partials(
        [partials[s] for s in range(chips)], last, score_weight, tok_len, heads, group
    )
    packed = jnp.sum(jnp.where(kept_here, shares[None], 0.0), 1)
    total = packed
    for s in range(1, zs):
        total = total + flip(packed, "tensor", s, zs)
    total = total.reshape(chips, 2, CAPR, tok_len)
    here = pick(total, core, 1)
    there = flip(pick(total, 1 - core, 1), "core", 1, 2)
    both = jnp.where(core == 0, jnp.stack([here, there], 1), jnp.stack([there, here], 1))
    leaving = by_flip(both, chip)
    arriving = [leaving[0]]
    for s in range(1, chips):
        arriving.append(flip(leaving[s], "chip", s, chips))
    values = by_flip(jnp.stack(arriving), chip)

    summed = add_up(exchange(output_terms(gathered, wo, zs), "tensor"))
    state = (state.astype(F32) + summed).astype(BF16)
    outputs.append(own_features(state))
    return jnp.stack(outputs), values.reshape(1, shards * CAPR, tok_len)


def solution(mesh):
    dp, tensor = mesh.shape["dp"], mesh.shape["tensor"]
    fine = Mesh(mesh.devices.reshape(dp // 2, 2, tensor), ("chip", "core", "tensor"))
    rows = ("chip", "core")
    every = ("chip", "core", "tensor")

    return jax.shard_map(
        per_device,
        mesh=fine,
        in_specs=(
            P(None, every),
            P(rows, "tensor"),
            P(rows, "tensor", None),
            P("tensor", rows),
            P(rows, None, "tensor", None),
            P(rows),
            P(rows, None, None),
            P(rows),
            P(rows, None),
            P(rows, "tensor"),
            P(rows, "tensor", None),
            P("tensor"),
        ),
        out_specs=(P(None, None, every), P(rows, None, None)),
        check_vma=False,
    )
```
